512 devices in a mesh: expert: 32 (over z_hi, x, core), row: 4 (over z_lo), col: 4 (over y).
Axes of the slice: x: 4, y: 4, z: 16 (z_hi: 4, z_lo: 4; z = z_hi * 4 + z_lo), core: 2. Of those that a mesh axis runs over, the one named last changes fastest.
Arguments:
- tokens: bfloat16 [32768, 3584], P(('expert', 'col'), 'row'), may hold values from -6 to 6
- slots: int32 [128, 6, 32, 2], P(('expert', 'col')), may hold values from 0 to 255
- counts: int32 [6, 32], replicated, may hold values from 1 to 256, as said below
- owner: int32 [32], replicated, may hold values from 0 to 31, each once
Outputs:
- moments: float32 [32, 3584, 3584], P('expert', 'row', 'col')
The draws below stay inside these ranges and needn't reach their ends.
Inputs may be any that keep to these rules, and one draw needn't show every extreme that they name: `counts`: in every panel at least one expert's count is 256.
All inputs are finite; a program needn't handle non-finite values.
Results may differ from the reference program's by a relative error of at most 0.0003.
Values may be sent and summed in bfloat16 or wider, within the bound.
No kernel may reach another device: no remote copies, remote signals or barrier semaphores. Data moves between devices by JAX's collectives and lax.ppermute only.
A program may use at most 64 MiB of HBM per device.

```python
import jax
import jax.numpy as jnp
from jax import lax

W = 3584
SLOT = 2
TOK_DEV = 256
PANELS = 6
EXPERTS = 32
PANEL_ROWS = 256
TOKENS = 32768
N_EXPERT = 32
N_COL = 4


def draw_counts(key, part):
    first_key = jax.random.fold_in(key, 11)
    second_key = jax.random.fold_in(key, 23)
    base_counts = jax.random.randint(first_key, (PANELS, EXPERTS), 1, PANEL_ROWS + 1)
    hottest = jax.random.randint(second_key, (PANELS,), 0, EXPERTS)
    column = jnp.arange(EXPERTS, dtype=jnp.int32)[None, :]
    return jnp.where(column == hottest[:, None], PANEL_ROWS, base_counts).astype(jnp.int32)


def touch_ends(result, own_key, smallest, high):
    shape = result.shape
    spot = [jax.random.randint(jax.random.fold_in(own_key, axis), (), 0, shape[axis]) for axis in range(len(shape))]
    result = result.at[tuple(spot)].set(smallest)
    longest = shape.index(max(shape))
    spot[longest] = (spot[longest] + 1) % shape[longest]
    return result.at[tuple(spot)].set(high)


def levels(rng, extent, shards, low, top_value):
    level, own = 1.0, jax.random.fold_in(rng, 6)
    for dim, parts in shards:
        heights = jnp.exp(jax.random.uniform(jax.random.fold_in(own, dim), (parts,), jnp.float32, low / len(shards), top_value / len(shards)))
        level = level * jnp.repeat(heights, extent[dim] // parts).reshape([-1 if axis == dim else 1 for axis in range(len(extent))])
    return level


def noise(own_key, extent, deviation, bound, cuts=(), held_as=jnp.bfloat16):
    entries = deviation * jax.random.normal(own_key, extent, jnp.float32)
    if cuts:
        entries = entries * levels(own_key, extent, cuts, -0.22, 0.18)
    return jnp.clip(entries, -bound, bound).astype(held_as)


def setup_inputs(seed: int = 0) -> dict:
    key_of = jax.random.split(jax.random.key(seed), 5)
    tokens = noise(key_of[0], (TOKENS, W), 1.0, 6.0, ((0, 128), (1, 4)))
    slots = touch_ends(jax.random.randint(key_of[1], (N_EXPERT * N_COL, PANELS, EXPERTS, SLOT), 0, TOK_DEV), jax.random.fold_in(key_of[1], 1), 0, TOK_DEV - 1).astype(jnp.int32)
    counts = draw_counts(jax.random.fold_in(key_of[4], 71), 0)
    owner = jax.random.permutation(key_of[3], EXPERTS).astype(jnp.int32)
    return {"tokens": tokens, "slots": slots, "counts": counts, "owner": owner}


def reference(tokens, slots, counts, owner):
    inverse = jnp.argsort(owner).astype(jnp.int32)

    def one_group(group):
        expert_id = inverse[group]
        local = jnp.take(slots, expert_id, axis=2)
        local = jnp.transpose(local, (1, 0, 2)).reshape(PANELS, PANEL_ROWS)
        position = jnp.arange(PANEL_ROWS, dtype=jnp.int32)
        global_rows = ((position // SLOT) * TOK_DEV)[None, :] + local
        usable = position[None, :] < jnp.take(counts, expert_id, axis=1)[:, None]
        picked = tokens[global_rows.reshape(-1).astype(jnp.int32)]
        picked = jnp.where(usable.reshape(-1)[:, None], picked, jnp.zeros_like(picked))
        moment = jnp.dot(picked.T, picked, preferred_element_type=jnp.float32)
        row_total = jnp.sum(jnp.take(counts, expert_id, axis=1)).astype(jnp.float32)
        return moment / row_total

    return lax.map(one_group, jnp.arange(EXPERTS, dtype=jnp.int32))
```

```python
import jax
import jax.numpy as jnp
from jax import lax
from jax.sharding import PartitionSpec as P

SIDE = 4


def shift_col(rows, step):
    return lax.ppermute(rows, "col", [(c, (c + step) % SIDE) for c in range(SIDE)])


def left_by_shift(rows):
    half = rows.shape[0] // 2
    plus, minus = shift_col(rows, 1), shift_col(rows, -1)
    far = jnp.concatenate([shift_col(plus[:half], 1), shift_col(minus[half:], -1)])
    return [rows, plus, far, minus]


def right_direct(rows, k):
    pairs = [(r * SIDE + c, ((c + k) % SIDE) * SIDE + r) for r in range(SIDE) for c in range(SIDE)]
    return lax.ppermute(rows, ("row", "col"), pairs)


def routed_rows(tokens, slots, counts, owner):
    groups = owner.shape[0]
    panels, slot_count = slots.shape[1], slots.shape[3]
    block = lax.axis_index("expert") * lax.axis_size("col") + lax.axis_index("col")
    mine = (owner[None, :] == jnp.arange(groups, dtype=jnp.int32)[:, None]).astype(jnp.float32)
    position = block * slot_count + jnp.arange(slot_count, dtype=jnp.int32)
    usable = position[None, None, :] < counts[:, :, None]
    table = jnp.where(usable, slots[0], -1).astype(jnp.float32)
    table = jnp.transpose(table, (1, 0, 2)).reshape(groups, panels * slot_count)
    picks = jnp.dot(mine, table, precision=lax.Precision.HIGHEST).astype(jnp.int32)
    hot = picks.reshape(-1, 1) == jnp.arange(tokens.shape[0], dtype=jnp.int32)[None, :]
    rows = jnp.dot(hot.astype(tokens.dtype), tokens, preferred_element_type=jnp.float32).astype(tokens.dtype)
    totals = jnp.sum(jnp.where(owner == lax.axis_index("expert"), counts, 0)).astype(jnp.float32)
    return rows.reshape(groups, panels * slot_count, tokens.shape[1]), totals


def per_device(tokens, slots, counts, owner):
    outgoing, total = routed_rows(tokens, slots, counts, owner)
    rows = lax.all_to_all(outgoing, "expert", 0, 0, tiled=True).reshape(-1, tokens.shape[1])
    r, c = lax.axis_index("row"), lax.axis_index("col")
    lefts = jnp.stack(left_by_shift(rows))
    tile = None
    for k in range(SIDE):
        right = right_direct(rows, k)
        left = lax.dynamic_index_in_dim(lefts, (c - r + k + SIDE) % SIDE, 0, keepdims=False)
        part = lax.dot_general(left, right, (((0,), (0,)), ((), ())), preferred_element_type=jnp.float32)
        tile = part if tile is None else tile + part
    return (tile / total)[None]


def solution(mesh):
    return jax.shard_map(
        per_device,
        mesh=mesh,
        in_specs=(P(("expert", "col"), "row"), P(("expert", "col"), None, None, None), P(), P()),
        out_specs=P("expert", "row", "col"),
        check_vma=False,
    )
```

```python
import jax
import jax.numpy as jnp
from jax import lax
from jax.sharding import PartitionSpec as P

SIDE = 4
SEGMENTS = 4
CHIPS = 8


def swap(rows, axis, mask):
    return lax.ppermute(rows, axis, [(i, i ^ mask) for i in range(SIDE)])


def routed_rows(tokens, slots, counts, owner):
    groups = owner.shape[0]
    panels, slot_count = slots.shape[1], slots.shape[3]
    block = lax.axis_index("expert") * lax.axis_size("col") + lax.axis_index("col")
    place = jnp.arange(groups, dtype=jnp.int32)
    segment = lax.axis_index("expert") // CHIPS
    group = ((place % SEGMENTS) ^ segment) * CHIPS + place // SEGMENTS
    mine = (owner[None, :] == group[:, None]).astype(jnp.float32)
    position = block * slot_count + jnp.arange(slot_count, dtype=jnp.int32)
    usable = position[None, None, :] < counts[:, :, None]
    table = jnp.where(usable, slots[0], -1).astype(jnp.float32)
    table = jnp.transpose(table, (1, 0, 2)).reshape(groups, panels * slot_count)
    picks = jnp.dot(mine, table, precision=lax.Precision.HIGHEST).astype(jnp.int32)
    hot = picks.reshape(-1, 1) == jnp.arange(tokens.shape[0], dtype=jnp.int32)[None, :]
    rows = jnp.dot(hot.astype(tokens.dtype), tokens, preferred_element_type=jnp.float32).astype(tokens.dtype)
    totals = jnp.sum(jnp.where(owner == lax.axis_index("expert"), counts, 0)).astype(jnp.float32)
    return rows.reshape(groups, panels * slot_count, tokens.shape[1]), totals


def moment_parts(rows):
    lefts = [rows] + [swap(rows, "col", m) for m in (1, 3, 2)]
    far = swap(rows, "row", 2)
    near = swap(rows, "row", 1)
    features = [rows, near, far, swap(far, "row", 1)]
    here = lax.axis_index("row") ^ lax.axis_index("col")
    picked = [pick(features, here ^ m) for m in (0, 1, 3, 2)]
    rights = [picked[0]] + [swap(q, "col", m) for q, m in zip(picked[1:], (1, 3, 2))]
    return list(zip(lefts, rights))


def pick(choices, index):
    chosen = choices[0]
    for i in range(1, len(choices)):
        chosen = jnp.where(index == i, choices[i], chosen)
    return chosen


def reach(rows, d):
    return lax.ppermute(rows, "expert", [(e, e ^ (d * CHIPS)) for e in range(SEGMENTS * CHIPS)])


def per_device(tokens, slots, counts, owner):
  outgoing, total = routed_rows(tokens, slots, counts, owner)
  width = tokens.shape[1]
  near_groups = [[z * CHIPS + i for i in range(CHIPS)] for z in range(SEGMENTS)]
  mixed = lax.all_to_all(outgoing.reshape(CHIPS, -1, width), "expert", 0, 0, tiled=True, axis_index_groups=near_groups)
  each = mixed.shape[1] // SEGMENTS
  pieces = [mixed[:, d * each : (d + 1) * each].reshape(-1, width) for d in range(SEGMENTS)]
  pieces = [pieces[0]] + [reach(pieces[d], d) for d in range(1, SEGMENTS)]
  tile = None
  for group in ((0, 1), (3, 2)):
      part = jnp.concatenate([pieces[d] for d in group])
      for left, right in moment_parts(part):
          term = lax.dot_general(left, right, (((0,), (0,)), ((), ())), preferred_element_type=jnp.float32)
          tile = term if tile is None else tile + term
  return (tile / total)[None]


def solution(mesh):
    return jax.shard_map(
        per_device,
        mesh=mesh,
        in_specs=(P(("expert", "col"), "row"), P(("expert", "col"), None, None, None), P(), P()),
        out_specs=P("expert", "row", "col"),
        check_vma=False,
    )
```

```python
import jax
import jax.numpy as jnp
from jax import lax
from jax.sharding import PartitionSpec as P

SIDE = 4
SEGMENTS = 4
CHIPS = 8


def swap(rows, axis, mask):
    return lax.ppermute(rows, axis, [(i, i ^ mask) for i in range(SIDE)])


def routed_rows(tokens, slots, counts, owner):
    groups = owner.shape[0]
    panels, slot_count = slots.shape[1], slots.shape[3]
    block = lax.axis_index("expert") * lax.axis_size("col") + lax.axis_index("col")
    place = jnp.arange(groups, dtype=jnp.int32)
    segment = lax.axis_index("expert") // CHIPS
    group = ((place % SEGMENTS) ^ segment) * CHIPS + place // SEGMENTS
    mine = (owner[None, :] == group[:, None]).astype(jnp.float32)
    position = block * slot_count + jnp.arange(slot_count, dtype=jnp.int32)
    usable = position[None, None, :] < counts[:, :, None]
    table = jnp.where(usable, slots[0], -1).astype(jnp.float32)
    table = jnp.transpose(table, (1, 0, 2)).reshape(groups, panels * slot_count)
    picks = jnp.dot(mine, table, precision=lax.Precision.HIGHEST).astype(jnp.int32)
    hot = picks.reshape(-1, 1) == jnp.arange(tokens.shape[0], dtype=jnp.int32)[None, :]
    rows = jnp.dot(hot.astype(tokens.dtype), tokens, preferred_element_type=jnp.float32).astype(tokens.dtype)
    totals = jnp.sum(jnp.where(owner == lax.axis_index("expert"), counts, 0)).astype(jnp.float32)
    return rows.reshape(groups, panels * slot_count, tokens.shape[1]), totals


def direct_parts(rows):
    lefts = [rows] + [swap(rows, "col", m) for m in (1, 2, 3)]
    out = []
    for k in range(SIDE):
        pairs = [(l * SIDE + c, (c ^ l ^ k) * SIDE + l) for l in range(SIDE) for c in range(SIDE)]
        out.append((pick(lefts, lax.axis_index("row") ^ k), lax.ppermute(rows, ("row", "col"), pairs)))
    return out


def pick(choices, index):
    chosen = choices[0]
    for i in range(1, len(choices)):
        chosen = jnp.where(index == i, choices[i], chosen)
    return chosen


def reach(rows, d):
    return lax.ppermute(rows, "expert", [(e, e ^ (d * CHIPS)) for e in range(SEGMENTS * CHIPS)])


def per_device(tokens, slots, counts, owner):
  outgoing, total = routed_rows(tokens, slots, counts, owner)
  width = tokens.shape[1]
  near_groups = [[z * CHIPS + i for i in range(CHIPS)] for z in range(SEGMENTS)]
  mixed = lax.all_to_all(outgoing.reshape(CHIPS, -1, width), "expert", 0, 0, tiled=True, axis_index_groups=near_groups)
  each = mixed.shape[1] // SEGMENTS
  pieces = [mixed[:, d * each : (d + 1) * each].reshape(-1, width) for d in range(SEGMENTS)]
  pieces = [pieces[0]] + [reach(pieces[d], d) for d in range(1, SEGMENTS)]
  tile = None
  for group in ((0, 1), (3, 2)):
      part = jnp.concatenate([pieces[d] for d in group])
      for left, right in (direct_parts)(part):
          term = lax.dot_general(left, right, (((0,), (0,)), ((), ())), preferred_element_type=jnp.float32)
          tile = term if tile is None else tile + term
  return (tile / total)[None]


def solution(mesh):
    return jax.shard_map(
        per_device,
        mesh=mesh,
        in_specs=(P(("expert", "col"), "row"), P(("expert", "col"), None, None, None), P(), P()),
        out_specs=P("expert", "row", "col"),
        check_vma=False,
    )
```

```python
import jax
import jax.numpy as jnp
from jax import lax
from jax.sharding import PartitionSpec as P

SIDE = 4
SEGMENTS = 4
CHIPS = 8


def swap(rows, axis, mask):
    return lax.ppermute(rows, axis, [(i, i ^ mask) for i in range(SIDE)])


def routed_rows(tokens, slots, counts, owner):
    groups = owner.shape[0]
    panels, slot_count = slots.shape[1], slots.shape[3]
    block = lax.axis_index("expert") * lax.axis_size("col") + lax.axis_index("col")
    place = jnp.arange(groups, dtype=jnp.int32)
    segment = lax.axis_index("expert") // CHIPS
    group = ((place % SEGMENTS) ^ segment) * CHIPS + place // SEGMENTS
    mine = (owner[None, :] == group[:, None]).astype(jnp.float32)
    position = block * slot_count + jnp.arange(slot_count, dtype=jnp.int32)
    usable = position[None, None, :] < counts[:, :, None]
    table = jnp.where(usable, slots[0], -1).astype(jnp.float32)
    table = jnp.transpose(table, (1, 0, 2)).reshape(groups, panels * slot_count)
    picks = jnp.dot(mine, table, precision=lax.Precision.HIGHEST).astype(jnp.int32)
    hot = picks.reshape(-1, 1) == jnp.arange(tokens.shape[0], dtype=jnp.int32)[None, :]
    rows = jnp.dot(hot.astype(tokens.dtype), tokens, preferred_element_type=jnp.float32).astype(tokens.dtype)
    totals = jnp.sum(jnp.where(owner == lax.axis_index("expert"), counts, 0)).astype(jnp.float32)
    return rows.reshape(groups, panels * slot_count, tokens.shape[1]), totals


def direct_parts(rows):
    lefts = [rows] + [swap(rows, "col", m) for m in (1, 2, 3)]
    out = []
    for k in range(SIDE):
        pairs = [(l * SIDE + c, (c ^ l ^ k) * SIDE + l) for l in range(SIDE) for c in range(SIDE) if c != k]
        right = lax.ppermute(rows, ("row", "col"), pairs)
        left = pick(lefts, lax.axis_index("row") ^ k)
        out.append((left, jnp.where(lax.axis_index("row") == lax.axis_index("col"), left, right)))
    return out


def pick(choices, index):
    chosen = choices[0]
    for i in range(1, len(choices)):
        chosen = jnp.where(index == i, choices[i], chosen)
    return chosen


def reach(rows, d):
    return lax.ppermute(rows, "expert", [(e, e ^ (d * CHIPS)) for e in range(SEGMENTS * CHIPS)])


def per_device(tokens, slots, counts, owner):
  outgoing, total = routed_rows(tokens, slots, counts, owner)
  width = tokens.shape[1]
  near_groups = [[z * CHIPS + i for i in range(CHIPS)] for z in range(SEGMENTS)]
  mixed = lax.all_to_all(outgoing.reshape(CHIPS, -1, width), "expert", 0, 0, tiled=True, axis_index_groups=near_groups)
  each = mixed.shape[1] // SEGMENTS
  pieces = [mixed[:, d * each : (d + 1) * each].reshape(-1, width) for d in range(SEGMENTS)]
  pieces = [pieces[0]] + [reach(pieces[d], d) for d in range(1, SEGMENTS)]
  tile = None
  for group in ((0, 1), (3, 2)):
      part = jnp.concatenate([pieces[d] for d in group])
      for left, right in (direct_parts)(part):
          term = lax.dot_general(left, right, (((0,), (0,)), ((), ())), preferred_element_type=jnp.float32)
          tile = term if tile is None else tile + term
  return (tile / total)[None]


def solution(mesh):
    return jax.shard_map(
        per_device,
        mesh=mesh,
        in_specs=(P(("expert", "col"), "row"), P(("expert", "col"), None, None, None), P(), P()),
        out_specs=P("expert", "row", "col"),
        check_vma=False,
    )
```
